512 devices in a mesh: user: 32 (over x_lo, z), item: 16 (over y, x_hi, core).
Axes of the slice: x: 4 (x_hi: 2, x_lo: 2; x = x_hi * 2 + x_lo), y: 4, z: 16, core: 2. Of those that a mesh axis runs over, the one named last changes fastest.
Arguments:
- xtiles: bfloat16 [32, 384, 256, 256], P('user', 'item'), may hold values from -6 to 6
- row_bits: int32 [32, 384, 8], P('user', 'item'), may hold values from -2147483648 to 2147483646
- col_bits: int32 [32, 384, 8], P('user', 'item'), may hold values from -2147483648 to 2147483646
- tile_row: int32 [32, 384], P('user', 'item'), may hold values from 0 to 1
- tile_col: int32 [32, 384], P('user', 'item'), may hold values from 0 to 15, as said below
- tile_count: int32 [32, 16], P('user', 'item'), may hold values from 1 to 24, as said below
- user_panel: bfloat16 [16384, 256], P('user'), may hold values from -0.375 to 0.375
- item_panel: bfloat16 [4096, 256], P('item'), may hold values from -6 to 6
- test_panel: bfloat16 [4096, 256], P('item'), may hold values from -0.0546875 to 0.0546875
Outputs:
- sketch: float32 [16384, 256], P('user')
- second_sketch: float32 [16, 256, 256], P('item', 'user')
The draws below stay inside these ranges and needn't reach their ends.
Inputs may be any that keep to these rules, and one draw needn't show every extreme that they name: `tile_col`: the item block of slot j on user index u is j // 24 - 1, j // 24 or j // 24 + 1, taken modulo 16. `tile_count`: some device has all 24 slots live.
All inputs are finite; a program needn't handle non-finite values.
Results may differ from the reference program's by a relative error of at most 0.0022.
Values may be sent and summed in bfloat16 or wider, within the bound.
No kernel may reach another device: no remote copies, remote signals or barrier semaphores. Data moves between devices by JAX's collectives and lax.ppermute only.
A program may use at most 64 MiB of HBM per device.

```python
import math
import jax
import jax.numpy as jnp
from jax import lax

BS = 256
K = 256
S = 256
RB = 2
TPD = 24
NU = 16384
NI = 4096
N_USER = 32
N_ITEM = 16


def draw_tile_col(key, part):
    home_block = jnp.arange(N_ITEM * TPD, dtype=jnp.int32) // TPD
    offsets = jax.random.randint(key, (N_USER, N_ITEM * TPD), -1, 2, dtype=jnp.int32)
    return (home_block[None, :] + offsets + N_ITEM) % N_ITEM


def draw_tile_count(key, part):
    first_key, second_key = jax.random.split(key)
    counts = jax.random.randint(first_key, (N_USER * N_ITEM,), 1, TPD + 1, dtype=jnp.int32)
    chosen = jax.random.randint(second_key, (), 0, N_USER * N_ITEM, dtype=jnp.int32)
    positions = jnp.arange(N_USER * N_ITEM, dtype=jnp.int32)
    counts = jnp.where(positions == chosen, TPD, counts)
    return counts.reshape(N_USER, N_ITEM)


def set_ends(values, key, smallest, largest):
    shape = values.shape
    spot = [jax.random.randint(jax.random.fold_in(key, axis), (), 0, shape[axis]) for axis in range(len(shape))]
    values = values.at[tuple(spot)].set(smallest)
    longest = shape.index(max(shape))
    spot[longest] = (spot[longest] + 1) % shape[longest]
    return values.at[tuple(spot)].set(largest)


def block_scale(own_key, shape, cuts, smallest, largest):
    gain = 1.0
    for position, blocks in cuts:
        steps = jax.random.uniform(jax.random.fold_in(jax.random.fold_in(own_key, 6), position), (blocks,), jnp.float32, smallest / len(cuts), largest / len(cuts))
        gain = gain * jnp.repeat(jnp.exp(steps), shape[position] // blocks).reshape((-1,) + (1,) * (len(shape) - 1 - position))
    return gain


def scatter_about(stream_key, dims, width, most, cuts=(), held_as=jnp.bfloat16):
    array = width * jax.random.normal(stream_key, dims, jnp.float32)
    if cuts:
        array = array * block_scale(stream_key, dims, cuts, -0.22, 0.18)
    return jnp.clip(array, -most, most).astype(held_as)


def setup_inputs(seed: int = 0) -> dict:
    streams_of = jax.random.split(jax.random.key(seed), 10)
    xtiles = scatter_about(streams_of[0], (N_USER, N_ITEM * TPD, BS, BS), 1.0, 6.0, ((0, 32), (1, 16)))
    row_bits = set_ends(jax.random.randint(streams_of[1], (N_USER, N_ITEM * TPD, BS // 32), -2147483648, 2147483647), jax.random.fold_in(streams_of[1], 1), -2147483648, 2147483646).astype(jnp.int32)
    col_bits = set_ends(jax.random.randint(streams_of[2], (N_USER, N_ITEM * TPD, BS // 32), -2147483648, 2147483647), jax.random.fold_in(streams_of[2], 1), -2147483648, 2147483646).astype(jnp.int32)
    tile_row = set_ends(jax.random.randint(streams_of[3], (N_USER, N_ITEM * TPD), 0, RB), jax.random.fold_in(streams_of[3], 1), 0, RB - 1).astype(jnp.int32)
    tile_col = draw_tile_col(jax.random.fold_in(streams_of[9], 71), 0)
    tile_count = draw_tile_count(jax.random.fold_in(streams_of[9], 71), 0)
    user_panel = scatter_about(streams_of[6], (NU, K), K ** -0.5, 0.375, ((0, 32),))
    item_panel = scatter_about(streams_of[7], (NI, K), 1.0, 6.0, ((0, 16),))
    test_panel = scatter_about(streams_of[8], (NI, S), (N_ITEM * TPD * BS // (4 * RB)) ** -0.5, 0.0546875, ((0, 16),))
    return dict(xtiles=xtiles, row_bits=row_bits, col_bits=col_bits, tile_row=tile_row, tile_col=tile_col, tile_count=tile_count, user_panel=user_panel, item_panel=item_panel, test_panel=test_panel)


def unpack(packed):
    offsets = jnp.arange(32, dtype=jnp.int32)
    bit_values = jnp.right_shift(packed[..., None], offsets) & 1
    return bit_values.reshape(packed.shape[:-1] + (packed.shape[-1] * 32,)).astype(jnp.float32)

def reference(xtiles, row_bits, col_bits, tile_row, tile_col, tile_count, user_panel, item_panel, test_panel):
    user_blocks = user_panel.reshape(N_USER, RB, BS, K)
    item_blocks = item_panel.reshape(N_ITEM, BS, K).astype(jnp.float32)
    test_blocks = test_panel.reshape(N_ITEM, BS, S).astype(jnp.float32)
    slot_ids = jnp.arange(N_ITEM * TPD, dtype=jnp.int32)

    def residual_rows(inputs):
        tile_data, row_packed, col_packed, row_ids, col_ids, counts, user_rows = inputs
        live_slots = (slot_ids % TPD < counts[slot_ids // TPD]).astype(jnp.float32)
        observed = unpack(row_packed)[:, :, None] * unpack(col_packed)[:, None, :] * live_slots[:, None, None]
        predicted = jnp.einsum('tak,tbk->tab', user_rows[row_ids].astype(jnp.float32), item_blocks[col_ids])
        residue = (observed * (tile_data.astype(jnp.float32) - predicted)).astype(jnp.bfloat16)
        sketch_tiles = jnp.einsum('tab,tbs->tas', residue.astype(jnp.float32), test_blocks[col_ids])
        return (residue, jax.ops.segment_sum(sketch_tiles, row_ids, num_segments=RB))
    residue, sketch = lax.map(residual_rows, (xtiles, row_bits, col_bits, tile_row, tile_col, tile_count, user_blocks))
    sketch_half = sketch.astype(jnp.bfloat16)

    def column_sums(running, inputs):
        residue_user, row_ids, col_ids, sketch_user = inputs
        column_tiles = jnp.einsum('tab,tas->tbs', residue_user.astype(jnp.float32), sketch_user[row_ids].astype(jnp.float32))
        return (running + jax.ops.segment_sum(column_tiles, col_ids, num_segments=N_ITEM), None)
    zero_sums = jnp.zeros((N_ITEM, BS, S), jnp.float32)
    running, _ = lax.scan(column_sums, zero_sums, (residue, tile_row, tile_col, sketch_half))
    sketch_scale = 2.0 / math.sqrt(N_USER * TPD * BS)
    return (sketch.reshape(N_USER * RB * BS, S), running * sketch_scale)
```

```python
import math

import jax
import jax.numpy as jnp
from jax import lax
from jax.experimental import pallas as pl
from jax.experimental.pallas import tpu as pltpu
from jax.sharding import PartitionSpec as P

WORD = 32
CHUNK = 4
VMEM_BYTES = 40 * 1024 * 1024
NT = (((1,), (1,)), ((), ()))


def cross_of(i, size):
    return (i + 1) % size if i % 2 else (i - 1) % size


def split(x):
    high = x.astype(jnp.bfloat16)
    return high, (x - high.astype(jnp.float32)).astype(jnp.bfloat16)


def residue_kernel(
    row_bits_ref, col_bits_ref, tile_row_ref, tile_col_ref, tile_count, user_ref,
    own_item, pair_item, cross_item, own_test, pair_test, cross_test, tiles_ref,
    sketch_ref, own_sum, mate_sum, cross_sum,
    row_bits, col_bits, tile_row, tile_col, users, items, tests, tiles, predicted, sums,
    tile_sems, table_sems, user_sem, item_sems, test_sems,
):
    slots, size, _ = tiles.shape
    chunks = slots // CHUNK
    blocks = users.shape[0] // size
    own = lax.axis_index("item")
    other = 1 - own % 2

    def fetch(c):
        part = pl.ds(c * CHUNK, CHUNK)
        return pltpu.make_async_copy(tiles_ref.at[part], tiles.at[part], tile_sems.at[c])

    user_load = pltpu.make_async_copy(user_ref, users, user_sem)
    item_loads = [
        pltpu.make_async_copy(source, items.at[k], item_sems.at[k])
        for k, source in enumerate((own_item, pair_item.at[other], cross_item))
    ]
    table_loads = [
        pltpu.make_async_copy(source, target, table_sems.at[k])
        for k, (source, target) in enumerate(
            (
                (row_bits_ref, row_bits), (col_bits_ref, col_bits), (tile_row_ref, tile_row),
                (tile_col_ref, tile_col),
            )
        )
    ]
    test_loads = [
        pltpu.make_async_copy(source, tests.at[k], test_sems.at[k])
        for k, source in enumerate((own_test, pair_test.at[other], cross_test))
    ]
    for load in (user_load, *item_loads, *table_loads):
        load.start()
    for c in range(chunks):
        fetch(c).start()
    for load in test_loads:
        load.start()
    sums[...] = jnp.zeros_like(sums)
    user_load.wait()
    for k in range(3):
        item_loads[k].wait()
        for r in range(blocks):
            predicted[3 * r + k] = lax.dot_general(
                users[r * size : (r + 1) * size, :], items[k], NT, preferred_element_type=jnp.float32
            )
    for load in table_loads:
        load.wait()
    live = tile_count[0, 0]
    lane = lax.broadcasted_iota(jnp.int32, (1, size), 1)
    place = jnp.left_shift(jnp.int32(1), lax.broadcasted_iota(jnp.int32, (WORD, size), 0))

    def one(t):
        block = tile_col[0, t]
        kind = jnp.where(block == own, 0, jnp.where(block // 2 == own // 2, 1, 2))
        which = 3 * tile_row[0, t] + kind
        words = jnp.zeros((1, size), jnp.int32)
        for w in range(size // WORD):
            words = jnp.where(lane // WORD == w, col_bits[w, t], words)
        seen = jnp.right_shift(words, lane % WORD) & 1
        marks = jnp.where(jnp.broadcast_to(seen, place.shape) != 0, place, 0)
        for w in range(size // WORD):
            rows = pl.ds(w * WORD, WORD)
            word = jnp.where(t < live, row_bits[w, t], 0)
            gap = (tiles[t, rows, :].astype(jnp.float32) - predicted[which, rows, :]).astype(jnp.bfloat16)
            sums[which, rows, :] += jnp.where((marks & word) != 0, gap.astype(jnp.float32), 0.0)

    @pl.loop(0, chunks)
    def _(c):
        fetch(c).wait()
        for k in range(CHUNK):
            one(c * CHUNK + k)

    for load in test_loads:
        load.wait()
    for r in range(blocks):
        total = jnp.zeros((size, tests.shape[2]), jnp.float32)
        for k in range(3):
            high, low = split(sums[3 * r + k])
            if k == 2:
                cross_sum[r] = high
            total += jnp.dot(high, tests[k], preferred_element_type=jnp.float32)
            total += jnp.dot(low, tests[k], preferred_element_type=jnp.float32)
        sketch_ref[r * size : (r + 1) * size, :] = total
        own_sum[r] = sums[3 * r]
        mate_sum[r] = sums[3 * r + 1]


def column_kernel(scale, half_ref, own_sum, mate_sum, cross_sum, out_ref):
    blocks, size, _ = own_sum.shape
    across = lax.broadcasted_iota(jnp.int32, (size, size), 0) == lax.broadcasted_iota(jnp.int32, (size, size), 1)
    unit = across.astype(jnp.float32).astype(jnp.bfloat16)
    total = jnp.zeros((half_ref.shape[1], size), jnp.float32)
    for r in range(blocks):
        turned = lax.dot_general(
            unit, half_ref[r * size : (r + 1) * size, :], NT, preferred_element_type=jnp.float32
        ).astype(jnp.bfloat16)
        high, low = split(own_sum[r] + mate_sum[r] + cross_sum[r].astype(jnp.float32))
        total += jnp.dot(turned, high, preferred_element_type=jnp.float32)
        total += jnp.dot(turned, low, preferred_element_type=jnp.float32)
    out_ref[...] = total.T.astype(jnp.bfloat16)


def shards(xtiles, row_bits, col_bits, tile_row, tile_col, tile_count, user_panel, item_panel, test_panel):
    size, rank = item_panel.shape
    width = test_panel.shape[1]
    rows = user_panel.shape[0]
    slots = xtiles.shape[1]
    blocks = rows // size
    users, items = lax.axis_size("user"), lax.axis_size("item")
    f32, b16, i32 = jnp.float32, jnp.bfloat16, jnp.int32
    pairs = [[i, i + 1] for i in range(0, items, 2)]
    mates = [(i, i + 1 - 2 * (i % 2)) for i in range(items)]
    crosses = [(i, cross_of(i, items)) for i in range(items)]
    half_way = users // 2
    far_crosses = [
        (u * items + i, (u + half_way) % users * items + cross_of(i, items))
        for u in range(users) for i in range(items)
    ]
    vmem = pl.BlockSpec(memory_space=pltpu.VMEM)
    hbm = pl.BlockSpec(memory_space=pl.ANY)

    def keep(x):
        return pltpu.with_memory_space_constraint(x, pltpu.HBM)

    cross_item = lax.ppermute(item_panel, ("user", "item"), far_crosses)
    cross_test = lax.ppermute(test_panel, ("user", "item"), far_crosses)
    pair_item = lax.all_gather(item_panel, "item", axis_index_groups=pairs)
    pair_test = lax.all_gather(test_panel, "item", axis_index_groups=pairs)

    words = row_bits.shape[2]
    partial_rows, own_sum, mate_sum, cross_sum = pl.pallas_call(
        residue_kernel,
        out_shape=(
            jax.ShapeDtypeStruct((rows, width), f32),
            jax.ShapeDtypeStruct((blocks, size, size), f32),
            jax.ShapeDtypeStruct((blocks, size, size), f32),
            jax.ShapeDtypeStruct((blocks, size, size), b16),
        ),
        in_specs=[hbm] * 4 + [pl.BlockSpec(memory_space=pltpu.SMEM)] + [hbm] * 8,
        out_specs=(vmem,) * 4,
        scratch_shapes=[
            pltpu.SMEM((words, slots), i32),
            pltpu.SMEM((words, slots), i32),
            pltpu.SMEM((1, slots), i32),
            pltpu.SMEM((1, slots), i32),
            pltpu.VMEM((rows, rank), b16),
            pltpu.VMEM((3, size, rank), b16),
            pltpu.VMEM((3, size, width), b16),
            pltpu.VMEM((slots, size, size), b16),
            pltpu.VMEM((3 * blocks, size, size), f32),
            pltpu.VMEM((3 * blocks, size, size), f32),
            pltpu.SemaphoreType.DMA((slots // CHUNK,)),
            pltpu.SemaphoreType.DMA((4,)),
            pltpu.SemaphoreType.DMA,
            pltpu.SemaphoreType.DMA((3,)),
            pltpu.SemaphoreType.DMA((3,)),
        ],
        compiler_params=pltpu.CompilerParams(vmem_limit_bytes=VMEM_BYTES),
    )(
        keep(row_bits[0].T), keep(col_bits[0].T), keep(tile_row), keep(tile_col), tile_count, keep(user_panel),
        keep(item_panel), pair_item, cross_item, keep(test_panel), pair_test, cross_test, keep(xtiles[0]),
    )
    from_cross = lax.ppermute(cross_sum, "item", crosses)
    from_mate = lax.ppermute(mate_sum, "item", mates)

    share = rows // items
    terms = lax.all_to_all(partial_rows.reshape(items, share, width), "item", 0, 0)
    own_half = terms.sum(0).astype(b16)
    half = lax.all_to_all(jnp.broadcast_to(own_half[None], terms.shape), "item", 0, 0).reshape(rows, width)

    scale = 2.0 / math.sqrt(users * slots * size)
    own_terms = pl.pallas_call(
        lambda *refs: column_kernel(scale, *refs),
        out_shape=jax.ShapeDtypeStruct((size, width), b16),
        in_specs=[vmem] * 4,
        out_specs=vmem,
        compiler_params=pltpu.CompilerParams(vmem_limit_bytes=VMEM_BYTES),
    )(half, own_sum, from_mate, from_cross)
    parts = lax.all_to_all(own_terms.reshape(users, size // users, width), "user", 0, 0)
    column_sum = parts.astype(f32).sum(0) * scale
    return (half.astype(f32), column_sum[None])


def solution(mesh):
    placed = (
        P("user", "item", None, None),
        P("user", "item", None),
        P("user", "item", None),
        P("user", "item"),
        P("user", "item"),
        P("user", "item"),
        P("user", None),
        P("item", None),
        P("item", None),
    )
    return jax.shard_map(
        shards,
        mesh=mesh,
        in_specs=placed,
        out_specs=(P("user", None), P("item", "user", None)),
        check_vma=False,
    )
```

```python
import math

import jax
import jax.numpy as jnp
from jax import lax
from jax.experimental import pallas as pl
from jax.experimental.pallas import tpu as pltpu
from jax.sharding import PartitionSpec as P

WORD = 32
CHUNK = 4
UNROLL = 2
VMEM_BYTES = 40 * 1024 * 1024
NT = (((1,), (1,)), ((), ()))


def cross_of(i, size):
    return (i + 1) % size if i % 2 else (i - 1) % size


def split(x):
    high = x.astype(jnp.bfloat16)
    return high, (x - high.astype(jnp.float32)).astype(jnp.bfloat16)


def join_kernel(item_ref, test_ref, out_ref, sems):
    size = item_ref.shape[0]
    loads = [
        pltpu.make_async_copy(source, out_ref.at[pl.ds(k * size, size)], sems.at[k])
        for k, source in enumerate((item_ref, test_ref))
    ]
    for load in loads:
        load.start()
    for load in loads:
        load.wait()


def table_copies(refs, scratch, sems):
    return [pltpu.make_async_copy(a, b, sems.at[k]) for k, (a, b) in enumerate(zip(refs, scratch, strict=True))]


def kind_of(block, own):
    return jnp.where(block == own, 0, jnp.where(block // 2 == own // 2, 1, 2))


def listed(order, live, wanted):
    def visit(t, found):
        order[found] = t
        return found + wanted(t).astype(jnp.int32)

    return lax.fori_loop(0, live, visit, jnp.int32(0))


def add_tiles(order, count, which_of, row_bits, col_bits, tiles, predicted, sums):
    slots, size, _ = tiles.shape
    lane = lax.broadcasted_iota(jnp.int32, (1, size), 1)
    place = jnp.left_shift(jnp.int32(1), lax.broadcasted_iota(jnp.int32, (WORD, size), 0))

    def one(j):
        on = j < count
        t = jnp.where(on, order[jnp.minimum(j, slots)], 0)
        which = which_of(t)
        words = jnp.zeros((1, size), jnp.int32)
        for w in range(size // WORD):
            words = jnp.where(lane // WORD == w, col_bits[w, t], words)
        seen = jnp.right_shift(words, lane % WORD) & 1
        marks = jnp.where(jnp.broadcast_to(seen, place.shape) != 0, place, 0)
        for w in range(size // WORD):
            rows = pl.ds(w * WORD, WORD)
            word = jnp.where(on, row_bits[w, t], 0)
            gap = (tiles[t, rows, :].astype(jnp.float32) - predicted[which, rows, :]).astype(jnp.bfloat16)
            sums[which, rows, :] += jnp.where((marks & word) != 0, gap.astype(jnp.float32), 0.0)

    @pl.loop(0, (count + UNROLL - 1) // UNROLL)
    def _(i):
        for k in range(UNROLL):
            one(UNROLL * i + k)


def chip_kernel(
    row_bits_ref, col_bits_ref, tile_row_ref, tile_col_ref, tile_count, user_ref, tiles_ref, pair,
    sketch_ref, own_sum, mate_sum, users, tiles,
    row_bits, col_bits, tile_row, tile_col, order, predicted, sums, tile_sems, table_sems, user_sem,
):
    slots, size, _ = tiles.shape
    blocks = users.shape[0] // size
    own = lax.axis_index("item")
    sides = (own % 2, 1 - own % 2)
    tables = table_copies(
        (row_bits_ref, col_bits_ref, tile_row_ref, tile_col_ref), (row_bits, col_bits, tile_row, tile_col), table_sems
    )
    user_load = pltpu.make_async_copy(user_ref, users, user_sem)
    tile_loads = [
        pltpu.make_async_copy(tiles_ref.at[pl.ds(c, CHUNK)], tiles.at[pl.ds(c, CHUNK)], tile_sems.at[c // CHUNK])
        for c in range(0, slots, CHUNK)
    ]
    for load in (user_load, *tables, *tile_loads):
        load.start()
    sums[...] = jnp.zeros_like(sums)
    user_load.wait()
    for k in range(2):
        for r in range(blocks):
            predicted[2 * r + k] = lax.dot_general(
                users[r * size : (r + 1) * size, :], pair[sides[k], :size, :], NT, preferred_element_type=jnp.float32
            )
    for load in tables:
        load.wait()
    count = listed(order, tile_count[0, 0], lambda t: kind_of(tile_col[0, t], own) < 2)
    for load in tile_loads:
        load.wait()
    add_tiles(
        order, count, lambda t: 2 * tile_row[0, t] + jnp.minimum(kind_of(tile_col[0, t], own), 1),
        row_bits, col_bits, tiles, predicted, sums,
    )
    for r in range(blocks):
        total = jnp.zeros((size, sketch_ref.shape[1]), jnp.float32)
        for k in range(2):
            high, low = split(sums[2 * r + k])
            test = pair[sides[k], size:, :]
            total += jnp.dot(high, test, preferred_element_type=jnp.float32)
            total += jnp.dot(low, test, preferred_element_type=jnp.float32)
        sketch_ref[r * size : (r + 1) * size, :] = total
        own_sum[r] = sums[2 * r]
        mate_sum[r] = sums[2 * r + 1]


def cross_kernel(
    row_bits_ref, col_bits_ref, tile_row_ref, tile_col_ref, tile_count, users, tiles, cross, chip_sketch,
    sketch_ref, cross_sum,
    row_bits, col_bits, tile_row, tile_col, order, predicted, sums, table_sems,
):
    size = tiles.shape[1]
    blocks = users.shape[0] // size
    own = lax.axis_index("item")
    tables = table_copies(
        (row_bits_ref, col_bits_ref, tile_row_ref, tile_col_ref), (row_bits, col_bits, tile_row, tile_col), table_sems
    )
    for load in tables:
        load.start()
    sums[...] = jnp.zeros_like(sums)
    for r in range(blocks):
        predicted[r] = lax.dot_general(
            users[r * size : (r + 1) * size, :], cross[:size, :], NT, preferred_element_type=jnp.float32
        )
    for load in tables:
        load.wait()
    count = listed(order, tile_count[0, 0], lambda t: kind_of(tile_col[0, t], own) == 2)
    add_tiles(order, count, lambda t: tile_row[0, t], row_bits, col_bits, tiles, predicted, sums)
    for r in range(blocks):
        high, low = split(sums[r])
        cross_sum[r] = high
        part = slice(r * size, (r + 1) * size)
        total = chip_sketch[part, :] + jnp.dot(high, cross[size:, :], preferred_element_type=jnp.float32)
        sketch_ref[part, :] = total + jnp.dot(low, cross[size:, :], preferred_element_type=jnp.float32)


def turn_kernel(own_sum, mate_sum, cross_sum, high_ref, low_ref):
    blocks, size, _ = own_sum.shape
    for r in range(blocks):
        part = slice(r * size, (r + 1) * size)
        high, low = split((own_sum[r] + mate_sum[r] + cross_sum[r].astype(jnp.float32)).T)
        high_ref[:, part] = high
        low_ref[:, part] = low


def column_kernel(half_ref, high_ref, low_ref, out_ref):
    half = half_ref[...]
    total = jnp.dot(high_ref[...], half, preferred_element_type=jnp.float32)
    total += jnp.dot(low_ref[...], half, preferred_element_type=jnp.float32)
    out_ref[...] = total.astype(jnp.bfloat16)


def shards(xtiles, row_bits, col_bits, tile_row, tile_col, tile_count, user_panel, item_panel, test_panel):
    size, rank = item_panel.shape
    width = test_panel.shape[1]
    rows = user_panel.shape[0]
    slots = xtiles.shape[1]
    blocks = rows // size
    users, items = lax.axis_size("user"), lax.axis_size("item")
    f32, b16, i32 = jnp.float32, jnp.bfloat16, jnp.int32
    pairs = [[i, i + 1] for i in range(0, items, 2)]
    mates = [(i, i + 1 - 2 * (i % 2)) for i in range(items)]
    crosses = [(i, cross_of(i, items)) for i in range(items)]
    half_way = users // 2
    far_crosses = [
        (u * items + i, (u + half_way) % users * items + cross_of(i, items))
        for u in range(users) for i in range(items)
    ]
    vmem = pl.BlockSpec(memory_space=pltpu.VMEM)
    hbm = pl.BlockSpec(memory_space=pl.ANY)

    def keep(x):
        return pltpu.with_memory_space_constraint(x, pltpu.HBM)

    params = pltpu.CompilerParams(vmem_limit_bytes=VMEM_BYTES)
    panels = pl.pallas_call(
        join_kernel,
        out_shape=pltpu.VMEM((2 * size, rank), b16),
        in_specs=[hbm, hbm],
        out_specs=vmem,
        scratch_shapes=[pltpu.SemaphoreType.DMA((2,))],
    )(keep(item_panel), keep(test_panel))
    cross = lax.ppermute(panels, ("user", "item"), far_crosses)
    pair = lax.all_gather(panels, "item", axis_index_groups=pairs)

    words = row_bits.shape[2]
    smem = pl.BlockSpec(memory_space=pltpu.SMEM)
    tables = (keep(row_bits[0].T), keep(col_bits[0].T), keep(tile_row), keep(tile_col), tile_count)
    table_specs = [hbm] * 4 + [smem]
    table_scratch = [
        pltpu.SMEM((words, slots), i32),
        pltpu.SMEM((words, slots), i32),
        pltpu.SMEM((1, slots), i32),
        pltpu.SMEM((1, slots), i32),
        pltpu.SMEM((slots + 1,), i32),
    ]
    sum_shape = jax.ShapeDtypeStruct((blocks, size, size), f32)
    chip_rows, own_sum, mate_sum, user_copy, tile_copy = pl.pallas_call(
        chip_kernel,
        out_shape=(
            jax.ShapeDtypeStruct((rows, width), f32),
            sum_shape,
            sum_shape,
            jax.ShapeDtypeStruct((rows, rank), b16),
            jax.ShapeDtypeStruct((slots, size, size), b16),
        ),
        in_specs=[*table_specs, hbm, hbm, vmem],
        out_specs=(vmem,) * 5,
        scratch_shapes=[
            *table_scratch,
            pltpu.VMEM((2 * blocks, size, size), f32),
            pltpu.VMEM((2 * blocks, size, size), f32),
            pltpu.SemaphoreType.DMA((slots // CHUNK,)),
            pltpu.SemaphoreType.DMA((4,)),
            pltpu.SemaphoreType.DMA,
        ],
        compiler_params=params,
    )(*tables, keep(user_panel), keep(xtiles[0]), pair)
    partial_rows, cross_sum = pl.pallas_call(
        cross_kernel,
        out_shape=(
            jax.ShapeDtypeStruct((rows, width), f32),
            jax.ShapeDtypeStruct((blocks, size, size), b16),
        ),
        in_specs=[*table_specs, vmem, vmem, vmem, vmem],
        out_specs=(vmem,) * 2,
        scratch_shapes=[
            *table_scratch,
            pltpu.VMEM((blocks, size, size), f32),
            pltpu.VMEM((blocks, size, size), f32),
            pltpu.SemaphoreType.DMA((4,)),
        ],
        compiler_params=params,
    )(*tables, user_copy, tile_copy, cross, chip_rows)
    from_cross = lax.ppermute(cross_sum, "item", crosses)
    from_mate = lax.ppermute(mate_sum, "item", mates)

    share = rows // items
    terms = lax.all_to_all(partial_rows.reshape(items, share, width), "item", 0, 0)
    own_half = terms.sum(0).astype(b16)
    half = lax.all_to_all(jnp.broadcast_to(own_half[None], terms.shape), "item", 0, 0).reshape(rows, width)

    scale = 2.0 / math.sqrt(users * slots * size)
    turned = jax.ShapeDtypeStruct((size, rows), b16)
    high, low = pl.pallas_call(
        turn_kernel,
        out_shape=(turned, turned),
        in_specs=[vmem] * 3,
        out_specs=(vmem, vmem),
        compiler_params=params,
    )(own_sum, from_mate, from_cross)
    own_terms = pl.pallas_call(
        column_kernel,
        out_shape=jax.ShapeDtypeStruct((size, width), b16),
        in_specs=[vmem] * 3,
        out_specs=vmem,
        compiler_params=params,
    )(half, high, low)
    parts = lax.all_to_all(own_terms.reshape(users, size // users, width), "user", 0, 0)
    column_sum = parts.astype(f32).sum(0) * scale
    return (half.astype(f32), column_sum[None])


def solution(mesh):
    placed = (
        P("user", "item", None, None),
        P("user", "item", None),
        P("user", "item", None),
        P("user", "item"),
        P("user", "item"),
        P("user", "item"),
        P("user", None),
        P("item", None),
        P("item", None),
    )
    return jax.shard_map(
        shards,
        mesh=mesh,
        in_specs=placed,
        out_specs=(P("user", None), P("item", "user", None)),
        check_vma=False,
    )
```

```python
import math

import jax
import jax.numpy as jnp
from jax import lax
from jax.experimental import pallas as pl
from jax.experimental.pallas import tpu as pltpu
from jax.sharding import PartitionSpec as P

WORD = 32
CHUNK = 4
UNROLL = 2
VMEM_BYTES = 40 * 1024 * 1024
NT = (((1,), (1,)), ((), ()))


def cross_of(i, size):
    return (i + 1) % size if i % 2 else (i - 1) % size


def split(x):
    high = x.astype(jnp.bfloat16)
    return high, (x - high.astype(jnp.float32)).astype(jnp.bfloat16)


def join_kernel(item_ref, test_ref, out_ref, sems):
    size = item_ref.shape[0]
    loads = [
        pltpu.make_async_copy(source, out_ref.at[pl.ds(k * size, size)], sems.at[k])
        for k, source in enumerate((item_ref, test_ref))
    ]
    for load in loads:
        load.start()
    for load in loads:
        load.wait()


def table_copies(refs, scratch, sems):
    return [pltpu.make_async_copy(a, b, sems.at[k]) for k, (a, b) in enumerate(zip(refs, scratch, strict=True))]


def kind_of(block, own):
    return jnp.where(block == own, 0, jnp.where(block // 2 == own // 2, 1, 2))


def listed(order, live, wanted):
    def visit(t, found):
        order[found] = t
        return found + wanted(t).astype(jnp.int32)

    return lax.fori_loop(0, live, visit, jnp.int32(0))


def add_tiles(order, count, which_of, row_bits, col_bits, tiles, predicted, sums):
    slots, size, _ = tiles.shape
    lane = lax.broadcasted_iota(jnp.int32, (1, size), 1)
    place = jnp.left_shift(jnp.int32(1), lax.broadcasted_iota(jnp.int32, (WORD, size), 0))

    def one(j):
        on = j < count
        t = jnp.where(on, order[jnp.minimum(j, slots)], 0)
        which = which_of(t)
        words = jnp.zeros((1, size), jnp.int32)
        for w in range(size // WORD):
            words = jnp.where(lane // WORD == w, col_bits[w, t], words)
        seen = jnp.right_shift(words, lane % WORD) & 1
        marks = jnp.where(jnp.broadcast_to(seen, place.shape) != 0, place, 0)
        for w in range(size // WORD):
            rows = pl.ds(w * WORD, WORD)
            word = jnp.where(on, row_bits[w, t], 0)
            gap = (tiles[t, rows, :].astype(jnp.float32) - predicted[which, rows, :]).astype(jnp.bfloat16)
            sums[which, rows, :] += jnp.where((marks & word) != 0, gap.astype(jnp.float32), 0.0)

    @pl.loop(0, (count + UNROLL - 1) // UNROLL)
    def _(i):
        for k in range(UNROLL):
            one(UNROLL * i + k)


def chip_kernel(
    row_bits_ref, col_bits_ref, tile_row_ref, tile_col_ref, tile_count, user_ref, tiles_ref, pair,
    sketch_ref, own_sum, mate_sum, users, tiles,
    row_bits, col_bits, tile_row, tile_col, order, predicted, sums, tile_sems, table_sems, user_sem,
):
    slots, size, _ = tiles.shape
    blocks = users.shape[0] // size
    own = lax.axis_index("item")
    sides = (own % 2, 1 - own % 2)
    tables = table_copies(
        (row_bits_ref, col_bits_ref, tile_row_ref, tile_col_ref), (row_bits, col_bits, tile_row, tile_col), table_sems
    )
    user_load = pltpu.make_async_copy(user_ref, users, user_sem)
    tile_loads = [
        pltpu.make_async_copy(tiles_ref.at[pl.ds(c, CHUNK)], tiles.at[pl.ds(c, CHUNK)], tile_sems.at[c // CHUNK])
        for c in range(0, slots, CHUNK)
    ]
    for load in (user_load, *tables, *tile_loads):
        load.start()
    sums[...] = jnp.zeros_like(sums)
    user_load.wait()
    for k in range(2):
        for r in range(blocks):
            predicted[2 * r + k] = lax.dot_general(
                users[r * size : (r + 1) * size, :], pair[sides[k], :size, :], NT, preferred_element_type=jnp.float32
            )
    for load in tables:
        load.wait()
    count = listed(order, tile_count[0, 0], lambda t: kind_of(tile_col[0, t], own) < 2)
    for load in tile_loads:
        load.wait()
    add_tiles(
        order, count, lambda t: 2 * tile_row[0, t] + jnp.minimum(kind_of(tile_col[0, t], own), 1),
        row_bits, col_bits, tiles, predicted, sums,
    )
    for r in range(blocks):
        total = jnp.zeros((size, sketch_ref.shape[1]), jnp.float32)
        for k in range(2):
            high, low = split(sums[2 * r + k])
            if k == 1:
                mate_sum[r] = high
            test = pair[sides[k], size:, :]
            total += jnp.dot(high, test, preferred_element_type=jnp.float32)
            total += jnp.dot(low, test, preferred_element_type=jnp.float32)
        sketch_ref[r * size : (r + 1) * size, :] = total
        own_sum[r] = sums[2 * r]


def cross_kernel(
    row_bits_ref, col_bits_ref, tile_row_ref, tile_col_ref, tile_count, users, tiles, cross, chip_sketch,
    kept_ref, sent_ref, cross_sum,
    row_bits, col_bits, tile_row, tile_col, order, predicted, sums, table_sems,
):
    size = tiles.shape[1]
    blocks = users.shape[0] // size
    own = lax.axis_index("item")
    tables = table_copies(
        (row_bits_ref, col_bits_ref, tile_row_ref, tile_col_ref), (row_bits, col_bits, tile_row, tile_col), table_sems
    )
    for load in tables:
        load.start()
    sums[...] = jnp.zeros_like(sums)
    for r in range(blocks):
        predicted[r] = lax.dot_general(
            users[r * size : (r + 1) * size, :], cross[:size, :], NT, preferred_element_type=jnp.float32
        )
    for load in tables:
        load.wait()
    count = listed(order, tile_count[0, 0], lambda t: kind_of(tile_col[0, t], own) == 2)
    add_tiles(order, count, lambda t: tile_row[0, t], row_bits, col_bits, tiles, predicted, sums)
    side = own % 2
    for r, out_ref in ((side, kept_ref), (1 - side, sent_ref)):
        high, low = split(sums[r])
        cross_sum[r] = high
        total = chip_sketch[pl.ds(pl.multiple_of(r * size, size), size), :]
        total += jnp.dot(high, cross[size:, :], preferred_element_type=jnp.float32)
        out_ref[...] = total + jnp.dot(low, cross[size:, :], preferred_element_type=jnp.float32)


def pair_kernel(kept_ref, pair_ref, out_ref):
    out_ref[...] = kept_ref[...] + pair_ref[1 - lax.axis_index("item") % 2]


def turn_kernel(own_sum, mate_sum, cross_sum, high_ref, low_ref):
    blocks, size, _ = own_sum.shape
    for r in range(blocks):
        part = slice(r * size, (r + 1) * size)
        high, low = split((own_sum[r] + mate_sum[r].astype(jnp.float32) + cross_sum[r].astype(jnp.float32)).T)
        high_ref[:, part] = high
        low_ref[:, part] = low


def column_kernel(half_ref, high_ref, low_ref, out_ref):
    chips, blocks, share, width = half_ref.shape
    size = chips * share
    total = jnp.zeros(out_ref.shape, jnp.float32)
    for r in range(blocks):
        half = half_ref[:, r].reshape(size, width)
        part = slice(r * size, (r + 1) * size)
        total += jnp.dot(high_ref[:, part], half, preferred_element_type=jnp.float32)
        total += jnp.dot(low_ref[:, part], half, preferred_element_type=jnp.float32)
    out_ref[...] = total.astype(jnp.bfloat16)


def spread_kernel(terms_ref, out_ref):
    half = jnp.sum(terms_ref[...], axis=0).astype(jnp.bfloat16)
    for k in range(out_ref.shape[0]):
        out_ref[k] = half


def shards(xtiles, row_bits, col_bits, tile_row, tile_col, tile_count, user_panel, item_panel, test_panel):
    size, rank = item_panel.shape
    width = test_panel.shape[1]
    rows = user_panel.shape[0]
    slots = xtiles.shape[1]
    blocks = rows // size
    users, items = lax.axis_size("user"), lax.axis_size("item")
    f32, b16, i32 = jnp.float32, jnp.bfloat16, jnp.int32
    pairs = [[i, i + 1] for i in range(0, items, 2)]
    mates = [(i, i + 1 - 2 * (i % 2)) for i in range(items)]
    crosses = [(i, cross_of(i, items)) for i in range(items)]
    half_way = users // 2
    far_crosses = [
        (u * items + i, (u + half_way) % users * items + cross_of(i, items))
        for u in range(users) for i in range(items)
    ]
    vmem = pl.BlockSpec(memory_space=pltpu.VMEM)
    hbm = pl.BlockSpec(memory_space=pl.ANY)

    def keep(x):
        return pltpu.with_memory_space_constraint(x, pltpu.HBM)

    params = pltpu.CompilerParams(vmem_limit_bytes=VMEM_BYTES)
    panels = pl.pallas_call(
        join_kernel,
        out_shape=pltpu.VMEM((2 * size, rank), b16),
        in_specs=[hbm, hbm],
        out_specs=vmem,
        scratch_shapes=[pltpu.SemaphoreType.DMA((2,))],
    )(keep(item_panel), keep(test_panel))
    cross = lax.ppermute(panels, ("user", "item"), far_crosses)
    pair = lax.all_gather(panels, "item", axis_index_groups=pairs)

    words = row_bits.shape[2]
    smem = pl.BlockSpec(memory_space=pltpu.SMEM)
    tables = (keep(row_bits[0].T), keep(col_bits[0].T), keep(tile_row), keep(tile_col), tile_count)
    table_specs = [hbm] * 4 + [smem]
    table_scratch = [
        pltpu.SMEM((words, slots), i32),
        pltpu.SMEM((words, slots), i32),
        pltpu.SMEM((1, slots), i32),
        pltpu.SMEM((1, slots), i32),
        pltpu.SMEM((slots + 1,), i32),
    ]
    chip_rows, own_sum, mate_sum, user_copy, tile_copy = pl.pallas_call(
        chip_kernel,
        out_shape=(
            jax.ShapeDtypeStruct((rows, width), f32),
            jax.ShapeDtypeStruct((blocks, size, size), f32),
            jax.ShapeDtypeStruct((blocks, size, size), b16),
            jax.ShapeDtypeStruct((rows, rank), b16),
            jax.ShapeDtypeStruct((slots, size, size), b16),
        ),
        in_specs=[*table_specs, hbm, hbm, vmem],
        out_specs=(vmem,) * 5,
        scratch_shapes=[
            *table_scratch,
            pltpu.VMEM((2 * blocks, size, size), f32),
            pltpu.VMEM((2 * blocks, size, size), f32),
            pltpu.SemaphoreType.DMA((slots // CHUNK,)),
            pltpu.SemaphoreType.DMA((4,)),
            pltpu.SemaphoreType.DMA,
        ],
        compiler_params=params,
    )(*tables, keep(user_panel), keep(xtiles[0]), pair)
    kept, sent, cross_sum = pl.pallas_call(
        cross_kernel,
        out_shape=(
            jax.ShapeDtypeStruct((size, width), f32),
            jax.ShapeDtypeStruct((size, width), f32),
            jax.ShapeDtypeStruct((blocks, size, size), b16),
        ),
        in_specs=[*table_specs, vmem, vmem, vmem, vmem],
        out_specs=(vmem,) * 3,
        scratch_shapes=[
            *table_scratch,
            pltpu.VMEM((blocks, size, size), f32),
            pltpu.VMEM((blocks, size, size), f32),
            pltpu.SemaphoreType.DMA((4,)),
        ],
        compiler_params=params,
    )(*tables, user_copy, tile_copy, cross, chip_rows)
    from_cross = lax.ppermute(cross_sum, "item", crosses)
    from_mate = lax.ppermute(mate_sum, "item", mates)

    chips = items // 2
    share = size // chips
    pair_terms = lax.all_gather(sent, "item", axis_index_groups=pairs)
    chip_terms = pl.pallas_call(
        pair_kernel,
        out_shape=jax.ShapeDtypeStruct((size, width), f32),
        in_specs=[vmem] * 2,
        out_specs=vmem,
        compiler_params=params,
    )(kept, pair_terms)
    same_core = [list(range(c, items, 2)) for c in range(2)]
    terms = lax.all_to_all(chip_terms.reshape(chips, share, width), "item", 0, 0, axis_index_groups=same_core)
    spread = pl.pallas_call(
        spread_kernel,
        out_shape=jax.ShapeDtypeStruct((items, share, width), b16),
        in_specs=[vmem],
        out_specs=vmem,
        compiler_params=params,
    )(terms)
    half = lax.all_to_all(spread, "item", 0, 0).reshape(chips, blocks, share, width)

    scale = 2.0 / math.sqrt(users * slots * size)
    turned = jax.ShapeDtypeStruct((size, rows), b16)
    high, low = pl.pallas_call(
        turn_kernel,
        out_shape=(turned, turned),
        in_specs=[vmem] * 3,
        out_specs=(vmem, vmem),
        compiler_params=params,
    )(own_sum, from_mate, from_cross)
    own_terms = pl.pallas_call(
        column_kernel,
        out_shape=jax.ShapeDtypeStruct((size, width), b16),
        in_specs=[vmem] * 3,
        out_specs=vmem,
        compiler_params=params,
    )(half, high, low)
    parts = lax.all_to_all(own_terms.reshape(users, size // users, width), "user", 0, 0)
    column_sum = parts.astype(f32).sum(0) * scale
    sketch = half.transpose(1, 0, 2, 3).reshape(rows, width).astype(f32)
    return (sketch, column_sum[None])


def solution(mesh):
    placed = (
        P("user", "item", None, None),
        P("user", "item", None),
        P("user", "item", None),
        P("user", "item"),
        P("user", "item"),
        P("user", "item"),
        P("user", None),
        P("item", None),
        P("item", None),
    )
    return jax.shard_map(
        shards,
        mesh=mesh,
        in_specs=placed,
        out_specs=(P("user", None), P("item", "user", None)),
        check_vma=False,
    )
```

```python
import functools
import math

import jax
import jax.numpy as jnp
from jax import lax
from jax.experimental import pallas as pl
from jax.experimental.pallas import tpu as pltpu
from jax.sharding import PartitionSpec as P

WORD = 32
CHUNK = 4
UNROLL = 2
VMEM_BYTES = 40 * 1024 * 1024
NT = (((1,), (1,)), ((), ()))
FIRST_USER = 26


def cross_of(i, size):
    return (i + 1) % size if i % 2 else (i - 1) % size


def split(x):
    high = x.astype(jnp.bfloat16)
    return high, (x - high.astype(jnp.float32)).astype(jnp.bfloat16)


def join_kernel(item_ref, test_ref, out_ref, sems):
    size = item_ref.shape[0]
    loads = [
        pltpu.make_async_copy(source, out_ref.at[pl.ds(k * size, size)], sems.at[k])
        for k, source in enumerate((item_ref, test_ref))
    ]
    for load in loads:
        load.start()
    for load in loads:
        load.wait()


def table_copies(refs, scratch, sems):
    return [pltpu.make_async_copy(a, b, sems.at[k]) for k, (a, b) in enumerate(zip(refs, scratch, strict=True))]


def kind_of(block, own):
    return jnp.where(block == own, 0, jnp.where(block // 2 == own // 2, 1, 2))


def listed(order, live, wanted):
    def visit(t, found):
        order[found] = t
        return found + wanted(t).astype(jnp.int32)

    return lax.fori_loop(0, live, visit, jnp.int32(0))


def add_tiles(order, count, which_of, row_bits, col_bits, tiles, predicted, sums):
    slots, size, _ = tiles.shape
    lane = lax.broadcasted_iota(jnp.int32, (1, size), 1)
    place = jnp.left_shift(jnp.int32(1), lax.broadcasted_iota(jnp.int32, (WORD, size), 0))

    def one(j):
        on = j < count
        t = jnp.where(on, order[jnp.minimum(j, slots)], 0)
        which = which_of(t)
        words = jnp.zeros((1, size), jnp.int32)
        for w in range(size // WORD):
            words = jnp.where(lane // WORD == w, col_bits[w, t], words)
        seen = jnp.right_shift(words, lane % WORD) & 1
        marks = jnp.where(jnp.broadcast_to(seen, place.shape) != 0, place, 0)
        for w in range(size // WORD):
            rows = pl.ds(w * WORD, WORD)
            word = jnp.where(on, row_bits[w, t], 0)
            gap = (tiles[t, rows, :].astype(jnp.float32) - predicted[which, rows, :]).astype(jnp.bfloat16)
            sums[which, rows, :] += jnp.where((marks & word) != 0, gap.astype(jnp.float32), 0.0)

    @pl.loop(0, (count + UNROLL - 1) // UNROLL)
    def _(i):
        for k in range(UNROLL):
            one(UNROLL * i + k)


def chip_kernel(
    row_bits_ref, col_bits_ref, tile_row_ref, tile_col_ref, tile_count, user_ref, tiles_ref, pair,
    sketch_ref, own_sum, mate_sum, users, tiles,
    row_bits, col_bits, tile_row, tile_col, order, predicted, sums, tile_sems, table_sems, user_sem,
):
    slots, size, _ = tiles.shape
    blocks = users.shape[0] // size
    own = lax.axis_index("item")
    sides = (own % 2, 1 - own % 2)
    tables = table_copies(
        (row_bits_ref, col_bits_ref, tile_row_ref, tile_col_ref), (row_bits, col_bits, tile_row, tile_col), table_sems
    )
    user_load = pltpu.make_async_copy(user_ref, users, user_sem)
    tile_loads = [
        pltpu.make_async_copy(tiles_ref.at[pl.ds(c, CHUNK)], tiles.at[pl.ds(c, CHUNK)], tile_sems.at[c // CHUNK])
        for c in range(0, slots, CHUNK)
    ]
    for load in (user_load, *tables, *tile_loads):
        load.start()
    sums[...] = jnp.zeros_like(sums)
    user_load.wait()
    for k in range(2):
        for r in range(blocks):
            predicted[2 * r + k] = lax.dot_general(
                users[r * size : (r + 1) * size, :], pair[sides[k], :size, :], NT, preferred_element_type=jnp.float32
            )
    for load in tables:
        load.wait()
    count = listed(order, tile_count[0, 0], lambda t: kind_of(tile_col[0, t], own) < 2)
    for load in tile_loads:
        load.wait()
    add_tiles(
        order, count, lambda t: 2 * tile_row[0, t] + jnp.minimum(kind_of(tile_col[0, t], own), 1),
        row_bits, col_bits, tiles, predicted, sums,
    )
    for r in range(blocks):
        total = jnp.zeros((size, sketch_ref.shape[1]), jnp.float32)
        for k in range(2):
            high, low = split(sums[2 * r + k])
            if k == 1:
                mate_sum[r] = high
            test = pair[sides[k], size:, :]
            total += jnp.dot(high, test, preferred_element_type=jnp.float32)
            total += jnp.dot(low, test, preferred_element_type=jnp.float32)
        sketch_ref[r * size : (r + 1) * size, :] = total
        own_sum[r] = sums[2 * r]


def cross_kernel(
    row_bits_ref, col_bits_ref, tile_row_ref, tile_col_ref, tile_count, users, tiles, cross, chip_sketch,
    kept_ref, sent_ref, cross_sum,
    row_bits, col_bits, tile_row, tile_col, order, predicted, sums, table_sems,
):
    size = tiles.shape[1]
    blocks = users.shape[0] // size
    own = lax.axis_index("item")
    tables = table_copies(
        (row_bits_ref, col_bits_ref, tile_row_ref, tile_col_ref), (row_bits, col_bits, tile_row, tile_col), table_sems
    )
    for load in tables:
        load.start()
    sums[...] = jnp.zeros_like(sums)
    for r in range(blocks):
        predicted[r] = lax.dot_general(
            users[r * size : (r + 1) * size, :], cross[:size, :], NT, preferred_element_type=jnp.float32
        )
    for load in tables:
        load.wait()
    count = listed(order, tile_count[0, 0], lambda t: kind_of(tile_col[0, t], own) == 2)
    add_tiles(order, count, lambda t: tile_row[0, t], row_bits, col_bits, tiles, predicted, sums)
    side = own % 2
    for r, out_ref in ((side, kept_ref), (1 - side, sent_ref)):
        high, low = split(sums[r])
        cross_sum[r] = high
        total = chip_sketch[pl.ds(pl.multiple_of(r * size, size), size), :]
        total += jnp.dot(high, cross[size:, :], preferred_element_type=jnp.float32)
        out_ref[...] = total + jnp.dot(low, cross[size:, :], preferred_element_type=jnp.float32)


def pair_kernel(kept_ref, pair_ref, out_ref):
    out_ref[...] = kept_ref[...] + pair_ref[1 - lax.axis_index("item") % 2]


def turn_kernel(own_sum, mate_sum, cross_sum, high_ref, low_ref):
    blocks, size, _ = own_sum.shape
    for r in range(blocks):
        part = slice(r * size, (r + 1) * size)
        high, low = split((own_sum[r] + mate_sum[r].astype(jnp.float32) + cross_sum[r].astype(jnp.float32)).T)
        high_ref[:, part] = high
        low_ref[:, part] = low


def column_kernel(start, half_ref, high_ref, low_ref, out_ref):
    chips, blocks, share, width = half_ref.shape
    size = chips * share
    total = jnp.zeros(out_ref.shape, jnp.float32)
    for r in range(blocks):
        half = half_ref[:, blocks - 1 - r].reshape(size, width)
        part = slice(r * size, (r + 1) * size)
        total += jnp.dot(high_ref[:, part], half, preferred_element_type=jnp.float32)
        total += jnp.dot(low_ref[:, part], half, preferred_element_type=jnp.float32)
    out_ref[: size - start, :] = total[start:, :].astype(jnp.bfloat16)
    out_ref[size - start :, :] = total[:start, :].astype(jnp.bfloat16)


def spread_kernel(terms_ref, out_ref):
    half = jnp.sum(terms_ref[...], axis=0).astype(jnp.bfloat16)
    for k in range(out_ref.shape[0]):
        out_ref[k] = half


def shards(xtiles, row_bits, col_bits, tile_row, tile_col, tile_count, user_panel, item_panel, test_panel):
    size, rank = item_panel.shape
    width = test_panel.shape[1]
    rows = user_panel.shape[0]
    slots = xtiles.shape[1]
    blocks = rows // size
    users, items = lax.axis_size("user"), lax.axis_size("item")
    f32, b16, i32 = jnp.float32, jnp.bfloat16, jnp.int32
    pairs = [[i, i + 1] for i in range(0, items, 2)]
    mates = [(i, i + 1 - 2 * (i % 2)) for i in range(items)]
    crosses = [(i, cross_of(i, items)) for i in range(items)]
    half_way = users // 2
    far_crosses = [
        (u * items + i, (u + half_way) % users * items + cross_of(i, items))
        for u in range(users) for i in range(items)
    ]
    vmem = pl.BlockSpec(memory_space=pltpu.VMEM)
    hbm = pl.BlockSpec(memory_space=pl.ANY)

    def keep(x):
        return pltpu.with_memory_space_constraint(x, pltpu.HBM)

    params = pltpu.CompilerParams(vmem_limit_bytes=VMEM_BYTES)
    panels = pl.pallas_call(
        join_kernel,
        out_shape=pltpu.VMEM((2 * size, rank), b16),
        in_specs=[hbm, hbm],
        out_specs=vmem,
        scratch_shapes=[pltpu.SemaphoreType.DMA((2,))],
    )(keep(item_panel), keep(test_panel))
    cross = lax.ppermute(panels, ("user", "item"), far_crosses)
    pair = lax.all_gather(panels, "item", axis_index_groups=pairs)

    words = row_bits.shape[2]
    smem = pl.BlockSpec(memory_space=pltpu.SMEM)
    tables = (keep(row_bits[0].T), keep(col_bits[0].T), keep(tile_row), keep(tile_col), tile_count)
    table_specs = [hbm] * 4 + [smem]
    table_scratch = [
        pltpu.SMEM((words, slots), i32),
        pltpu.SMEM((words, slots), i32),
        pltpu.SMEM((1, slots), i32),
        pltpu.SMEM((1, slots), i32),
        pltpu.SMEM((slots + 1,), i32),
    ]
    chip_rows, own_sum, mate_sum, user_copy, tile_copy = pl.pallas_call(
        chip_kernel,
        out_shape=(
            jax.ShapeDtypeStruct((rows, width), f32),
            jax.ShapeDtypeStruct((blocks, size, size), f32),
            jax.ShapeDtypeStruct((blocks, size, size), b16),
            jax.ShapeDtypeStruct((rows, rank), b16),
            jax.ShapeDtypeStruct((slots, size, size), b16),
        ),
        in_specs=[*table_specs, hbm, hbm, vmem],
        out_specs=(vmem,) * 5,
        scratch_shapes=[
            *table_scratch,
            pltpu.VMEM((2 * blocks, size, size), f32),
            pltpu.VMEM((2 * blocks, size, size), f32),
            pltpu.SemaphoreType.DMA((slots // CHUNK,)),
            pltpu.SemaphoreType.DMA((4,)),
            pltpu.SemaphoreType.DMA,
        ],
        compiler_params=params,
    )(*tables, keep(user_panel), keep(xtiles[0]), pair)
    kept, sent, cross_sum = pl.pallas_call(
        cross_kernel,
        out_shape=(
            jax.ShapeDtypeStruct((size, width), f32),
            jax.ShapeDtypeStruct((size, width), f32),
            jax.ShapeDtypeStruct((blocks, size, size), b16),
        ),
        in_specs=[*table_specs, vmem, vmem, vmem, vmem],
        out_specs=(vmem,) * 3,
        scratch_shapes=[
            *table_scratch,
            pltpu.VMEM((blocks, size, size), f32),
            pltpu.VMEM((blocks, size, size), f32),
            pltpu.SemaphoreType.DMA((4,)),
        ],
        compiler_params=params,
    )(*tables, user_copy, tile_copy, cross, chip_rows)
    from_cross = lax.ppermute(cross_sum, "item", crosses)
    from_mate = lax.ppermute(mate_sum, "item", mates)

    chips = items // 2
    share = size // chips
    pair_terms = lax.all_gather(sent, "item", axis_index_groups=pairs)
    chip_terms = pl.pallas_call(
        pair_kernel,
        out_shape=jax.ShapeDtypeStruct((size, width), f32),
        in_specs=[vmem] * 2,
        out_specs=vmem,
        compiler_params=params,
    )(kept, pair_terms)
    same_core = [list(range(c, items, 2)) for c in range(2)]
    terms = lax.all_to_all(chip_terms.reshape(chips, share, width), "item", 0, 0, axis_index_groups=same_core)
    spread = pl.pallas_call(
        spread_kernel,
        out_shape=jax.ShapeDtypeStruct((items, share, width), b16),
        in_specs=[vmem],
        out_specs=vmem,
        compiler_params=params,
    )(terms)
    swapped = [i + 1 - 2 * (i % 2) for i in range(items)]
    half = lax.all_to_all(spread, "item", 0, 0, axis_index_groups=[swapped]).reshape(chips, blocks, share, width)

    scale = 2.0 / math.sqrt(users * slots * size)
    turned = jax.ShapeDtypeStruct((size, rows), b16)
    high, low = pl.pallas_call(
        turn_kernel,
        out_shape=(turned, turned),
        in_specs=[vmem] * 3,
        out_specs=(vmem, vmem),
        compiler_params=params,
    )(own_sum, from_mate, from_cross)
    first = FIRST_USER % users
    own_terms = pl.pallas_call(
        functools.partial(column_kernel, first * (size // users)),
        out_shape=jax.ShapeDtypeStruct((size, width), b16),
        in_specs=[vmem] * 3,
        out_specs=vmem,
        compiler_params=params,
    )(half, high, low)
    turn = [(u + first) % users for u in range(users)]
    parts = lax.all_to_all(
        own_terms.reshape(users, size // users, width), "user", 0, 0, axis_index_groups=[turn]
    )
    column_sum = parts.astype(f32).sum(0) * scale
    sketch = half[:, ::-1].transpose(1, 0, 2, 3).reshape(rows, width).astype(f32)
    return (sketch, column_sum[None])


def solution(mesh):
    placed = (
        P("user", "item", None, None),
        P("user", "item", None),
        P("user", "item", None),
        P("user", "item"),
        P("user", "item"),
        P("user", "item"),
        P("user", None),
        P("item", None),
        P("item", None),
    )
    return jax.shard_map(
        shards,
        mesh=mesh,
        in_specs=placed,
        out_specs=(P("user", None), P("item", "user", None)),
        check_vma=False,
    )
```

```python
import functools
import math

import jax
import jax.numpy as jnp
from jax import lax
from jax.experimental import pallas as pl
from jax.experimental.pallas import tpu as pltpu
from jax.sharding import PartitionSpec as P

WORD = 32
CHUNK = 4
UNROLL = 2
VMEM_BYTES = 40 * 1024 * 1024
NT = (((1,), (1,)), ((), ()))
FIRST_USER = 10


def cross_of(i, size):
    return (i + 1) % size if i % 2 else (i - 1) % size


def split(x):
    high = x.astype(jnp.bfloat16)
    return high, (x - high.astype(jnp.float32)).astype(jnp.bfloat16)


def join_kernel(item_ref, test_ref, out_ref, sems):
    size = item_ref.shape[0]
    loads = [
        pltpu.make_async_copy(source, out_ref.at[pl.ds(k * size, size)], sems.at[k])
        for k, source in enumerate((item_ref, test_ref))
    ]
    for load in loads:
        load.start()
    for load in loads:
        load.wait()


def table_copies(refs, scratch, sems):
    return [pltpu.make_async_copy(a, b, sems.at[k]) for k, (a, b) in enumerate(zip(refs, scratch, strict=True))]


def kind_of(block, own):
    return jnp.where(block == own, 0, jnp.where(block // 2 == own // 2, 1, 2))


def listed(order, live, wanted):
    def visit(t, found):
        order[found] = t
        return found + wanted(t).astype(jnp.int32)

    return lax.fori_loop(0, live, visit, jnp.int32(0))


def add_tiles(order, count, which_of, row_bits, col_bits, tiles, predicted, sums):
    slots, size, _ = tiles.shape
    lane = lax.broadcasted_iota(jnp.int32, (1, size), 1)
    place = jnp.left_shift(jnp.int32(1), lax.broadcasted_iota(jnp.int32, (WORD, size), 0))

    def one(j):
        on = j < count
        t = jnp.where(on, order[jnp.minimum(j, slots)], 0)
        which = which_of(t)
        words = jnp.zeros((1, size), jnp.int32)
        for w in range(size // WORD):
            words = jnp.where(lane // WORD == w, col_bits[w, t], words)
        seen = jnp.right_shift(words, lane % WORD) & 1
        marks = jnp.where(jnp.broadcast_to(seen, place.shape) != 0, place, 0)
        for w in range(size // WORD):
            rows = pl.ds(w * WORD, WORD)
            word = jnp.where(on, row_bits[w, t], 0)
            gap = (tiles[t, rows, :].astype(jnp.float32) - predicted[which, rows, :]).astype(jnp.bfloat16)
            sums[which, rows, :] += jnp.where((marks & word) != 0, gap.astype(jnp.float32), 0.0)

    @pl.loop(0, (count + UNROLL - 1) // UNROLL)
    def _(i):
        for k in range(UNROLL):
            one(UNROLL * i + k)


def chip_kernel(
    row_bits_ref, col_bits_ref, tile_row_ref, tile_col_ref, tile_count, user_ref, tiles_ref, pair,
    sketch_ref, own_sum, mate_sum, users, tiles,
    row_bits, col_bits, tile_row, tile_col, order, predicted, sums, tile_sems, table_sems, user_sem,
):
    slots, size, _ = tiles.shape
    blocks = users.shape[0] // size
    own = lax.axis_index("item")
    sides = (1 - own % 2, own % 2)
    tables = table_copies(
        (row_bits_ref, col_bits_ref, tile_row_ref, tile_col_ref), (row_bits, col_bits, tile_row, tile_col), table_sems
    )
    user_load = pltpu.make_async_copy(user_ref, users, user_sem)
    tile_loads = [
        pltpu.make_async_copy(tiles_ref.at[pl.ds(c, CHUNK)], tiles.at[pl.ds(c, CHUNK)], tile_sems.at[c // CHUNK])
        for c in range(0, slots, CHUNK)
    ]
    for load in (user_load, *tables, *tile_loads):
        load.start()
    sums[...] = jnp.zeros_like(sums)
    user_load.wait()
    for k in range(2):
        for r in range(blocks):
            predicted[2 * r + k] = lax.dot_general(
                users[r * size : (r + 1) * size, :], pair[sides[k], :size, :], NT, preferred_element_type=jnp.float32
            )
    for load in tables:
        load.wait()
    count = listed(order, tile_count[0, 0], lambda t: kind_of(tile_col[0, t], own) < 2)
    for load in tile_loads:
        load.wait()
    add_tiles(
        order, count, lambda t: 2 * tile_row[0, t] + jnp.minimum(kind_of(tile_col[0, t], own), 1),
        row_bits, col_bits, tiles, predicted, sums,
    )
    for r in range(blocks):
        total = jnp.zeros((size, sketch_ref.shape[1]), jnp.float32)
        for k in range(2):
            high, low = split(sums[2 * r + k])
            if k == 1:
                mate_sum[r] = high
            test = pair[sides[k], size:, :]
            total += jnp.dot(high, test, preferred_element_type=jnp.float32)
            total += jnp.dot(low, test, preferred_element_type=jnp.float32)
        sketch_ref[r * size : (r + 1) * size, :] = total
        own_sum[r] = sums[2 * r]


def cross_kernel(
    row_bits_ref, col_bits_ref, tile_row_ref, tile_col_ref, tile_count, users, tiles, cross, chip_sketch,
    kept_ref, sent_ref, cross_sum,
    row_bits, col_bits, tile_row, tile_col, order, predicted, sums, table_sems,
):
    size = tiles.shape[1]
    blocks = users.shape[0] // size
    own = lax.axis_index("item")
    tables = table_copies(
        (row_bits_ref, col_bits_ref, tile_row_ref, tile_col_ref), (row_bits, col_bits, tile_row, tile_col), table_sems
    )
    for load in tables:
        load.start()
    sums[...] = jnp.zeros_like(sums)
    for r in range(blocks):
        predicted[r] = lax.dot_general(
            users[r * size : (r + 1) * size, :], cross[:size, :], NT, preferred_element_type=jnp.float32
        )
    for load in tables:
        load.wait()
    count = listed(order, tile_count[0, 0], lambda t: kind_of(tile_col[0, t], own) == 2)
    add_tiles(order, count, lambda t: tile_row[0, t], row_bits, col_bits, tiles, predicted, sums)
    side = own % 2
    for r, out_ref in ((side, kept_ref), (1 - side, sent_ref)):
        high, low = split(sums[r])
        cross_sum[r] = high
        total = chip_sketch[pl.ds(pl.multiple_of(r * size, size), size), :]
        total += jnp.dot(high, cross[size:, :], preferred_element_type=jnp.float32)
        out_ref[...] = total + jnp.dot(low, cross[size:, :], preferred_element_type=jnp.float32)


def pair_kernel(kept_ref, pair_ref, out_ref):
    out_ref[...] = kept_ref[...] + pair_ref[lax.axis_index("item") % 2]


def turn_kernel(own_sum, mate_sum, cross_sum, high_ref, low_ref):
    blocks, size, _ = own_sum.shape
    for r in range(blocks):
        part = slice(r * size, (r + 1) * size)
        high, low = split((own_sum[r] + mate_sum[r].astype(jnp.float32) + cross_sum[r].astype(jnp.float32)).T)
        high_ref[:, part] = high
        low_ref[:, part] = low


def column_kernel(start, half_ref, high_ref, low_ref, out_ref):
    chips, blocks, share, width = half_ref.shape
    size = chips * share
    total = jnp.zeros(out_ref.shape, jnp.float32)
    for r in range(blocks):
        half = half_ref[:, blocks - 1 - r].reshape(size, width)
        part = slice(r * size, (r + 1) * size)
        total += jnp.dot(high_ref[:, part], half, preferred_element_type=jnp.float32)
        total += jnp.dot(low_ref[:, part], half, preferred_element_type=jnp.float32)
    out_ref[: size - start, :] = total[start:, :].astype(jnp.bfloat16)
    out_ref[size - start :, :] = total[:start, :].astype(jnp.bfloat16)


def spread_kernel(terms_ref, out_ref):
    half = jnp.sum(terms_ref[...], axis=0).astype(jnp.bfloat16)
    for k in range(out_ref.shape[0]):
        out_ref[k] = half


def shards(xtiles, row_bits, col_bits, tile_row, tile_col, tile_count, user_panel, item_panel, test_panel):
    size, rank = item_panel.shape
    width = test_panel.shape[1]
    rows = user_panel.shape[0]
    slots = xtiles.shape[1]
    blocks = rows // size
    users, items = lax.axis_size("user"), lax.axis_size("item")
    f32, b16, i32 = jnp.float32, jnp.bfloat16, jnp.int32
    pairs = [[i + 1, i] for i in range(0, items, 2)]
    mates = [(i, i + 1 - 2 * (i % 2)) for i in range(items)]
    crosses = [(i, cross_of(i, items)) for i in range(items)]
    half_way = users // 2
    far_crosses = [
        (u * items + i, (u + half_way) % users * items + cross_of(i, items))
        for u in range(users) for i in range(items)
    ]
    vmem = pl.BlockSpec(memory_space=pltpu.VMEM)
    hbm = pl.BlockSpec(memory_space=pl.ANY)

    def keep(x):
        return pltpu.with_memory_space_constraint(x, pltpu.HBM)

    params = pltpu.CompilerParams(vmem_limit_bytes=VMEM_BYTES)
    panels = pl.pallas_call(
        join_kernel,
        out_shape=pltpu.VMEM((2 * size, rank), b16),
        in_specs=[hbm, hbm],
        out_specs=vmem,
        scratch_shapes=[pltpu.SemaphoreType.DMA((2,))],
    )(keep(item_panel), keep(test_panel))
    cross = lax.ppermute(panels, ("user", "item"), far_crosses)
    pair = lax.all_gather(panels, "item", axis_index_groups=pairs)

    words = row_bits.shape[2]
    smem = pl.BlockSpec(memory_space=pltpu.SMEM)
    tables = (keep(row_bits[0].T), keep(col_bits[0].T), keep(tile_row), keep(tile_col), tile_count)
    table_specs = [hbm] * 4 + [smem]
    table_scratch = [
        pltpu.SMEM((words, slots), i32),
        pltpu.SMEM((words, slots), i32),
        pltpu.SMEM((1, slots), i32),
        pltpu.SMEM((1, slots), i32),
        pltpu.SMEM((slots + 1,), i32),
    ]
    chip_rows, own_sum, mate_sum, user_copy, tile_copy = pl.pallas_call(
        chip_kernel,
        out_shape=(
            jax.ShapeDtypeStruct((rows, width), f32),
            jax.ShapeDtypeStruct((blocks, size, size), f32),
            jax.ShapeDtypeStruct((blocks, size, size), b16),
            jax.ShapeDtypeStruct((rows, rank), b16),
            jax.ShapeDtypeStruct((slots, size, size), b16),
        ),
        in_specs=[*table_specs, hbm, hbm, vmem],
        out_specs=(vmem,) * 5,
        scratch_shapes=[
            *table_scratch,
            pltpu.VMEM((2 * blocks, size, size), f32),
            pltpu.VMEM((2 * blocks, size, size), f32),
            pltpu.SemaphoreType.DMA((slots // CHUNK,)),
            pltpu.SemaphoreType.DMA((4,)),
            pltpu.SemaphoreType.DMA,
        ],
        compiler_params=params,
    )(*tables, keep(user_panel), keep(xtiles[0]), pair)
    kept, sent, cross_sum = pl.pallas_call(
        cross_kernel,
        out_shape=(
            jax.ShapeDtypeStruct((size, width), f32),
            jax.ShapeDtypeStruct((size, width), f32),
            jax.ShapeDtypeStruct((blocks, size, size), b16),
        ),
        in_specs=[*table_specs, vmem, vmem, vmem, vmem],
        out_specs=(vmem,) * 3,
        scratch_shapes=[
            *table_scratch,
            pltpu.VMEM((blocks, size, size), f32),
            pltpu.VMEM((blocks, size, size), f32),
            pltpu.SemaphoreType.DMA((4,)),
        ],
        compiler_params=params,
    )(*tables, user_copy, tile_copy, cross, chip_rows)
    from_cross = lax.ppermute(cross_sum, "item", crosses)
    from_mate = lax.ppermute(mate_sum, "item", mates)

    chips = items // 2
    share = size // chips
    pair_terms = lax.all_gather(sent, "item", axis_index_groups=pairs)
    chip_terms = pl.pallas_call(
        pair_kernel,
        out_shape=jax.ShapeDtypeStruct((size, width), f32),
        in_specs=[vmem] * 2,
        out_specs=vmem,
        compiler_params=params,
    )(kept, pair_terms)
    same_core = [list(range(c, items, 2)) for c in range(2)]
    terms = lax.all_to_all(chip_terms.reshape(chips, share, width), "item", 0, 0, axis_index_groups=same_core)
    spread = pl.pallas_call(
        spread_kernel,
        out_shape=jax.ShapeDtypeStruct((items, share, width), b16),
        in_specs=[vmem],
        out_specs=vmem,
        compiler_params=params,
    )(terms)
    swapped = [i + 1 - 2 * (i % 2) for i in range(items)]
    half = lax.all_to_all(spread, "item", 0, 0, axis_index_groups=[swapped]).reshape(chips, blocks, share, width)

    scale = 2.0 / math.sqrt(users * slots * size)
    turned = jax.ShapeDtypeStruct((size, rows), b16)
    high, low = pl.pallas_call(
        turn_kernel,
        out_shape=(turned, turned),
        in_specs=[vmem] * 3,
        out_specs=(vmem, vmem),
        compiler_params=params,
    )(own_sum, from_mate, from_cross)
    first = FIRST_USER % users
    own_terms = pl.pallas_call(
        functools.partial(column_kernel, first * (size // users)),
        out_shape=jax.ShapeDtypeStruct((size, width), b16),
        in_specs=[vmem] * 3,
        out_specs=vmem,
        compiler_params=params,
    )(half, high, low)
    turn = [(u + first) % users for u in range(users)]
    parts = lax.all_to_all(
        own_terms.reshape(users, size // users, width), "user", 0, 0, axis_index_groups=[turn]
    )
    column_sum = parts.astype(f32).sum(0) * scale
    sketch = half[:, ::-1].transpose(1, 0, 2, 3).reshape(rows, width).astype(f32)
    return (sketch, column_sum[None])


def solution(mesh):
    placed = (
        P("user", "item", None, None),
        P("user", "item", None),
        P("user", "item", None),
        P("user", "item"),
        P("user", "item"),
        P("user", "item"),
        P("user", None),
        P("item", None),
        P("item", None),
    )
    return jax.shard_map(
        shards,
        mesh=mesh,
        in_specs=placed,
        out_specs=(P("user", None), P("item", "user", None)),
        check_vma=False,
    )
```
